32 devices in a mesh: dp: 4 (over y, core), expert: 8 (over z, x).
Axes of the slice: x: 2, y: 2, z: 4, core: 2. Of those that a mesh axis runs over, the one named last changes fastest.
Arguments:
- tokens: bfloat16 [4096, 2048], P(('dp', 'expert')), may hold values from -6 to 6
- d_mixed: bfloat16 [4096, 2048], P(('dp', 'expert')), may hold values from -6 to 6
- w_in: bfloat16 [32, 2048, 768], P('expert'), may hold values from -0.125 to 0.125
- w_out: bfloat16 [32, 384, 2048], P('expert'), may hold values from -0.3125 to 0.3125
- expert_ids: int32 [4096, 8], P(('dp', 'expert')), may hold values from 0 to 31, all different within a row; in each aligned block of 128 rows (0 to 127, 128 to 255, ...) at most 40 rows name the same one
- gate_fixed: int32 [4096, 8], P(('dp', 'expert')), may hold values from 1 to 65535
- placement: int32 [32], replicated, may hold values from 0 to 31, each once
Outputs:
- mixed: bfloat16 [4096, 2048], P(('dp', 'expert'))
- d_tokens: bfloat16 [4096, 2048], P(('dp', 'expert'))
- grad_in: bfloat16 [32, 2048, 768], P('expert', 'dp')
- grad_out: bfloat16 [32, 384, 2048], P('expert', None, 'dp')
The draws below stay inside these ranges and needn't reach their ends.
Inputs may be any that keep to these rules, and one draw needn't show every extreme that they name: `expert_ids`: each row names 8 different experts. Among the rows of one device no expert is named more than 40 times, and in every draw some expert is named exactly 40 times by the rows of some device. Each number appears once: expert e's weights are in slot placement[e], held by expert-axis index placement[e] // 4.
All inputs are finite; a program needn't handle non-finite values.
Results may differ from the reference program's by a relative error of at most 0.009.
Values may be sent and summed in bfloat16 or wider, within the bound.
No kernel may reach another device: no remote copies, remote signals or barrier semaphores. Data moves between devices by JAX's collectives and lax.ppermute only.
A program may use at most 192 MiB of HBM per device.

```python
import math
import jax
import jax.numpy as jnp
import numpy as np
from jax import lax

D = 2048
FF = 384
TOP = 8
TOK_DEV = 128
EXPERTS = 32
TOKENS = 4096
CAP = 40
N_DP = 4
N_EXPERT = 8


def touch_ends(drawn, key, least, high):
    extent = drawn.shape
    place = [jax.random.randint(jax.random.fold_in(key, axis), (), 0, extent[axis]) for axis in range(len(extent))]
    drawn = drawn.at[tuple(place)].set(least)
    longest = extent.index(max(extent))
    place[longest] = (place[longest] + 1) % extent[longest]
    return drawn.at[tuple(place)].set(high)


def shard_levels(own_key, shape, shards, low, high):
    loudness, own = 1.0, jax.random.fold_in(own_key, 6)
    for dim, shards_of in shards:
        heights = jnp.exp(jax.random.uniform(jax.random.fold_in(own, dim), (shards_of,), jnp.float32, low / len(shards), high / len(shards)))
        loudness = loudness * jnp.repeat(heights, shape[dim] // shards_of).reshape([-1 if axis == dim else 1 for axis in range(len(shape))])
    return loudness


def shared_out(rng, own, number, rows, count, top, bound, skew):
    sequence = jax.random.permutation(rng, count)
    heavy_load, usual = portions_of(count, rows * top, bound, skew, True), portions_of(count, rows * top, bound, skew, False)
    places = jnp.arange(count)

    def named(sizes, turn):
        used = int((sizes > 0).sum())
        fixed = max(1, used // 4)
        passed = fixed + (places - fixed + turn * (used - fixed)) % max(1, count - fixed)
        return jnp.zeros((count,), jnp.int32).at[sequence[jnp.where(places < fixed, places, passed)]].set(jnp.asarray(sizes, jnp.int32))

    sizes = jnp.where(number % 4 == 0, named(heavy_load, number // 4), named(usual, number - number // 4 - 1))
    mixed = jax.random.permutation(jax.random.fold_in(own, 3), count)
    donor, receiver = mixed[0:count // 2 * 2:2], mixed[1:count // 2 * 2:2]
    margin = jnp.minimum(sizes[donor] - 1, bound - sizes[receiver]) // 2
    margin = jnp.where((donor == sequence[0]) | (receiver == sequence[0]) | (sizes[receiver] == 0), 0, jnp.maximum(margin, 0))
    passed = jax.random.randint(jax.random.fold_in(own, 4), (count // 2,), 0, 1 << 20) % (margin + 1)
    sizes = sizes.at[donor].add(-passed).at[receiver].add(passed)
    items = jnp.searchsorted(jnp.cumsum(sizes), jnp.arange(rows * top), side="right").astype(jnp.int32)
    grid = items.reshape(top, rows).T
    grid = grid[jax.random.permutation(jax.random.fold_in(own, 1), rows)]
    turn = jax.random.randint(jax.random.fold_in(own, 2), (rows, 1), 0, top)
    return jnp.take_along_axis(grid, (jnp.arange(top)[None, :] + turn) % top, axis=1)


def portions_of(amount, total, most, skew, full):
    weights = [(1 << 20) // math.isqrt(rank ** skew) + 1 for rank in range(1, amount + 1)]
    largest = most if full else min(most, max(-(-total // amount), total * weights[0] // sum(weights)))
    least = 1 if total - largest >= amount - 1 else 0
    holding, rest = [largest] + [least] * (amount - 1), total - largest - least * (amount - 1)
    while rest > 0:
        candidates = [i for i in range(1, amount) if holding[i] < largest] or [i for i in range(1, amount) if holding[i] < most]
        mass, budget = sum([weights[i] for i in candidates]), rest
        for i in candidates:
            addition = min(most - holding[i], max(1, budget * weights[i] // mass), rest)
            holding[i] = holding[i] + addition
            rest = rest - addition
    return np.array(holding)


def centred(own_key, extent, deviation, limit, shards=(), kind=jnp.bfloat16):
    drawn = jax.random.normal(own_key, extent, jnp.float32) * deviation
    if len(shards) > 0:
        drawn = shard_levels(own_key, extent, shards, -0.22, 0.18) * drawn
    return jnp.clip(drawn, min=-limit, max=limit).astype(kind)


def setup_inputs(seed: int = 0) -> dict:
    keys = jax.random.split(jax.random.key(seed), 8)
    tokens = centred(keys[0], (TOKENS, D), 1.0, 6.0, ((0, 32),))
    d_mixed = centred(keys[1], (TOKENS, D), 1.0, 6.0, ((0, 32),))
    w_in = centred(keys[2], (EXPERTS, D, 2 * FF), D ** -0.5, 0.125, ((0, 8),))
    w_out = centred(keys[3], (EXPERTS, FF, D), FF ** -0.5, 0.3125, ((0, 8),))
    expert_ids_keys = jax.random.split(jax.random.fold_in(keys[4], 1), TOKENS // TOK_DEV)
    expert_ids_turns = jax.random.permutation(jax.random.fold_in(keys[4], 3), TOKENS // TOK_DEV)
    expert_ids = jax.vmap(lambda own, number: shared_out(jax.random.fold_in(keys[4], 2), own, number, TOK_DEV, EXPERTS, TOP, CAP, 2))(expert_ids_keys, expert_ids_turns).reshape((TOKENS, TOP))
    gate_fixed = touch_ends(jax.random.randint(keys[5], (TOKENS, TOP), 1, 65536), jax.random.fold_in(keys[5], 1), 1, 65535).astype(jnp.int32)
    placement = jax.random.permutation(keys[6], EXPERTS).astype(jnp.int32)
    return {"tokens": tokens, "d_mixed": d_mixed, "w_in": w_in, "w_out": w_out, "expert_ids": expert_ids, "gate_fixed": gate_fixed, "placement": placement}


def reference(tokens, d_mixed, w_in, w_out, expert_ids, gate_fixed, placement):
    blocks = N_DP * N_EXPERT
    rows_slot = blocks * CAP
    gates = gate_fixed.astype(jnp.float32)
    gates = gates / jnp.sum(gates, axis=1, keepdims=True)
    slot = placement[expert_ids].astype(jnp.int32)
    block_slot = slot.reshape(blocks, TOK_DEV * TOP)
    catalog = jnp.arange(EXPERTS, dtype=jnp.int32)
    onehot = (block_slot[:, :, None] == catalog).astype(jnp.int32)
    rank = jnp.sum(jnp.cumsum(onehot, axis=1) * onehot, axis=2) - 1
    block_index = jnp.arange(blocks, dtype=jnp.int32)[:, None]
    dest = (block_slot * rows_slot + block_index * CAP + rank).astype(jnp.int32)
    dest = dest.reshape(TOKENS, TOP)
    token_index = jnp.broadcast_to(jnp.arange(TOKENS, dtype=jnp.int32)[:, None], (TOKENS, TOP))
    source = jnp.full((EXPERTS * rows_slot,), TOKENS, dtype=jnp.int32)
    source = source.at[dest.reshape(-1)].set(token_index.reshape(-1)).reshape(EXPERTS, rows_slot)
    slot_gate = jnp.zeros((EXPERTS * rows_slot,), jnp.float32)
    slot_gate = slot_gate.at[dest.reshape(-1)].set(gates.reshape(-1)).reshape(EXPERTS, rows_slot)
    zero_row = jnp.zeros((1, D), jnp.bfloat16)
    x_padded = jnp.concatenate([tokens, zero_row], axis=0)
    d_padded = jnp.concatenate([d_mixed, zero_row], axis=0)

    def one_slot(items):
        picks, slot_g, wi, wo = items
        rows = x_padded[picks]
        pre = jnp.dot(rows, wi, preferred_element_type=jnp.float32)
        gate = pre[:, :FF]
        up = pre[:, FF:]
        sig = jax.nn.sigmoid(gate)
        silu = gate * sig
        act = (silu * up).astype(jnp.bfloat16)
        out = jnp.dot(act, wo, preferred_element_type=jnp.float32).astype(jnp.bfloat16)
        d_exp = (slot_g[:, None] * d_padded[picks].astype(jnp.float32)).astype(jnp.bfloat16)
        d_act = jnp.dot(d_exp, wo.T, preferred_element_type=jnp.float32)
        d_gate = d_act * up * sig * (1.0 + gate * (1.0 - sig))
        d_up = d_act * silu
        d_pre = jnp.concatenate([d_gate, d_up], axis=1).astype(jnp.bfloat16)
        d_rows = jnp.dot(d_pre, wi.T, preferred_element_type=jnp.float32).astype(jnp.bfloat16)
        act_g = act.reshape(N_DP, -1, FF).astype(jnp.float32)
        dexp_g = d_exp.reshape(N_DP, -1, D).astype(jnp.float32)
        rows_g = rows.reshape(N_DP, -1, D).astype(jnp.float32)
        dpre_g = d_pre.reshape(N_DP, -1, 2 * FF).astype(jnp.float32)
        part_out = jnp.einsum('prf,prd->pfd', act_g, dexp_g).astype(jnp.bfloat16)
        part_in = jnp.einsum('prd,prf->pdf', rows_g, dpre_g).astype(jnp.bfloat16)
        part_out = lax.optimization_barrier(part_out)
        part_in = lax.optimization_barrier(part_in)
        g_out = jnp.sum(part_out.astype(jnp.float32), axis=0).astype(jnp.bfloat16)
        g_in = jnp.sum(part_in.astype(jnp.float32), axis=0).astype(jnp.bfloat16)
        return out, d_rows, g_in, g_out

    outs, d_all, grad_in, grad_out = lax.map(one_slot, (source, slot_gate, w_in, w_out))
    out_flat = outs.reshape(-1, D)
    d_flat = d_all.reshape(-1, D)
    mixed = jnp.zeros((TOKENS, D), jnp.float32)
    d_tokens = jnp.zeros((TOKENS, D), jnp.float32)
    for k in range(TOP):
        mixed = mixed + gates[:, k:k + 1] * out_flat[dest[:, k]].astype(jnp.float32)
        d_tokens = d_tokens + d_flat[dest[:, k]].astype(jnp.float32)
    return mixed.astype(jnp.bfloat16), d_tokens.astype(jnp.bfloat16), grad_in, grad_out
```

```python
import jax
import jax.numpy as jnp
from jax import lax
from jax.experimental import pallas as pl
from jax.experimental.pallas import tpu as pltpu
from jax.sharding import PartitionSpec as P

F32, BF16 = jnp.float32, jnp.bfloat16
LIMIT = 48 << 20


def ring_pairs(count):
    order = list(range(0, count, 2)) + list(range(count - 1 - count % 2, 0, -2))
    ahead = [(order[i], order[(i + 1) % count]) for i in range(count)]
    return ahead, [(b, a) for a, b in ahead]


def narrow(a):
    return a.astype(BF16)


def wide(a):
    return a.astype(F32)


def ring_gather(block, pairs):
    ahead, back = pairs
    half = block.shape[0] // 2
    f = g = block
    blocks = [block]
    for _ in range(1, len(ahead) // 2):
        f = lax.ppermute(f, "expert", ahead)
        g = lax.ppermute(g, "expert", back)
        blocks += [f, g]
    blocks.append(lax.ppermute(f[:half], "expert", ahead))
    blocks.append(lax.ppermute(g[half:], "expert", back))
    return blocks


def ring_scatter(parts, pairs):
    ahead, back = pairs
    count = len(ahead)
    half = parts[0].shape[0] // 2
    f = lax.ppermute(parts[-1][:half], "expert", ahead)
    g = lax.ppermute(parts[-1][half:], "expert", back)
    for step in range(count // 2 - 1, 0, -1):
        fwd, bwd = parts[2 * step], parts[2 * step - 1]
        if step == count // 2 - 1:
            fwd = jnp.concatenate([narrow(wide(fwd[:half]) + wide(f)), fwd[half:]])
            bwd = jnp.concatenate([bwd[:half], narrow(wide(bwd[half:]) + wide(g))])
        else:
            fwd, bwd = narrow(wide(fwd) + wide(f)), narrow(wide(bwd) + wide(g))
        f = lax.ppermute(fwd, "expert", ahead)
        g = lax.ppermute(bwd, "expert", back)
    return narrow(wide(parts[0]) + wide(f) + wide(g))


def dot(a, b, ca, cb):
    return lax.dot_general(a, b, (((ca,), (cb,)), ((), ())), preferred_element_type=F32)


def cost(flops, size):
    return pl.CostEstimate(flops=flops, bytes_accessed=size, transcendentals=0)


def forward(x, meta, held, w_in, slot, top):
    total, width = x.shape
    both = w_in.shape[2]
    hidden = both // 2
    tile = min(256, total)

    def kernel(held_ref, x_ref, meta_ref, w_ref, act_ref, lr_ref):
        m = wide(meta_ref[...])
        fixed = m[:, top : 2 * top] * 256.0 + m[:, 2 * top : 3 * top]
        gates = fixed / jnp.sum(fixed, axis=1, keepdims=True)
        hit = m[:, :top] == held_ref[slot].astype(F32)
        weight = jnp.sum(jnp.where(hit, gates, 0.0), axis=1, keepdims=True)
        pre = dot(x_ref[...], w_ref[0], 1, 0)
        gate, up = pre[:, :hidden], pre[:, hidden:]
        sig = jax.nn.sigmoid(gate)
        silu = gate * sig
        lean = weight * silu
        act_ref[...] = narrow(lean * up)
        lr_ref[:, :hidden] = narrow(weight * up * sig * (1.0 + gate * (1.0 - sig)))
        lr_ref[:, hidden:] = narrow(lean)

    row = lambda w: pl.BlockSpec((tile, w), lambda i: (i, 0))
    return pl.pallas_call(
        kernel,
        grid=(total // tile,),
        in_specs=[
            pl.BlockSpec(memory_space=pltpu.SMEM),
            row(width),
            row(meta.shape[1]),
            pl.BlockSpec((1, width, both), lambda i: (slot, 0, 0)),
        ],
        out_specs=[row(hidden), row(both)],
        out_shape=[
            jax.ShapeDtypeStruct((total, hidden), BF16),
            jax.ShapeDtypeStruct((total, both), BF16),
        ],
        compiler_params=pltpu.CompilerParams(vmem_limit_bytes=LIMIT),
        cost_estimate=cost(2 * total * width * both, 2 * width * (total + both)),
        name="forward",
    )(held, x, meta, w_in)


def mix(acts, w_out):
    slots, hidden, width = w_out.shape
    total = acts[0].shape[0]
    tile, cols = min(1024, total), min(512, width)

    def kernel(*refs):
        w_ref, out_ref = refs[slots], refs[slots + 1]
        acc = dot(refs[0][...], w_ref[0], 1, 0)
        for s in range(1, slots):
            acc = acc + dot(refs[s][...], w_ref[s], 1, 0)
        out_ref[...] = narrow(acc)

    return pl.pallas_call(
        kernel,
        grid=(total // tile, width // cols),
        in_specs=[pl.BlockSpec((tile, hidden), lambda r, j: (r, 0))] * slots
        + [pl.BlockSpec((slots, hidden, cols), lambda r, j: (0, 0, j))],
        out_specs=pl.BlockSpec((tile, cols), lambda r, j: (r, j)),
        out_shape=jax.ShapeDtypeStruct((total, width), BF16),
        compiler_params=pltpu.CompilerParams(vmem_limit_bytes=LIMIT),
        cost_estimate=cost(2 * total * width * slots * hidden, 2 * width * (total + slots * hidden)),
        name="mix",
    )(*acts, w_out)


def backward(d, lr, w_out, slot):
    total, width = d.shape
    both = lr.shape[1]
    hidden = both // 2
    tile = min(256, total)

    def kernel(d_ref, lr_ref, w_ref, out_ref):
        d_act = dot(d_ref[...], w_ref[0], 1, 1)
        out_ref[:, :hidden] = narrow(d_act * wide(lr_ref[:, :hidden]))
        out_ref[:, hidden:] = narrow(d_act * wide(lr_ref[:, hidden:]))

    row = lambda w: pl.BlockSpec((tile, w), lambda i: (i, 0))
    return pl.pallas_call(
        kernel,
        grid=(total // tile,),
        in_specs=[row(width), row(both), pl.BlockSpec((1, hidden, width), lambda i: (slot, 0, 0))],
        out_specs=row(both),
        out_shape=jax.ShapeDtypeStruct((total, both), BF16),
        compiler_params=pltpu.CompilerParams(vmem_limit_bytes=LIMIT),
        cost_estimate=cost(2 * total * width * hidden, 2 * width * (total + hidden)),
        name="backward",
    )(d, lr, w_out)


def gradients(x, d, act, d_pre, order, parts):
    total, width = x.shape
    hidden, both = act.shape[1], d_pre.shape[1]
    tile, part = min(1024, total), width // parts
    steps, half = total // tile, parts // 2

    def kernel(order_ref, x_ref, d_ref, act_ref, dp_ref, gi_a, go_a, gi_b, go_b, acc_in, acc_out):
        j, r = pl.program_id(0), pl.program_id(1)
        here_in = dot(x_ref[...], dp_ref[...], 0, 0)
        here_out = dot(act_ref[...], d_ref[...], 0, 0)

        def put(gi, go):
            if steps == 1:
                gi[0], go[0] = narrow(here_in), narrow(here_out)
                return

            @pl.when(r == steps - 1)
            def _():
                gi[0] = narrow(acc_in[...] + here_in)
                go[0] = narrow(acc_out[...] + here_out)

        if steps > 1:
            @pl.when(r == 0)
            def _():
                acc_in[...] = jnp.zeros_like(acc_in)
                acc_out[...] = jnp.zeros_like(acc_out)

        pl.when(j < half)(lambda: put(gi_a, go_a))
        pl.when(j >= half)(lambda: put(gi_b, go_b))
        if steps > 1:
            @pl.when(r < steps - 1)
            def _():
                acc_in[...] += here_in
                acc_out[...] += here_out

    first = lambda j, r, o: (jnp.minimum(j, half - 1), 0, 0)
    second = lambda j, r, o: (jnp.maximum(j - half, 0), 0, 0)
    cols = pl.BlockSpec((tile, part), lambda j, r, o: (r, o[j]))
    row = lambda w: pl.BlockSpec((tile, w), lambda j, r, o: (r, 0))
    spec_in = lambda m: pl.BlockSpec((1, part, both), m)
    spec_out = lambda m: pl.BlockSpec((1, hidden, part), m)
    shape_in = jax.ShapeDtypeStruct((half, part, both), BF16)
    shape_out = jax.ShapeDtypeStruct((half, hidden, part), BF16)
    return pl.pallas_call(
        kernel,
        grid_spec=pltpu.PrefetchScalarGridSpec(
            num_scalar_prefetch=1,
            grid=(parts, steps),
            in_specs=[cols, cols, row(hidden), row(both)],
            out_specs=[spec_in(first), spec_out(first), spec_in(second), spec_out(second)],
            scratch_shapes=[
                pltpu.VMEM((part, both) if steps > 1 else (8, 128), F32),
                pltpu.VMEM((hidden, part) if steps > 1 else (8, 128), F32),
            ],
        ),
        out_shape=[shape_in, shape_out, shape_in, shape_out],
        compiler_params=pltpu.CompilerParams(vmem_limit_bytes=LIMIT),
        cost_estimate=cost(2 * total * width * (both + hidden), 2 * width * (2 * total + both + hidden)),
        name="gradients",
    )(order, x, d, act, d_pre)


def rows_back(d_pres, w_in, start, count):
    slots, width, both = w_in.shape
    tile, cols = min(512, count), min(512, width)

    def kernel(*refs):
        w_ref, out_ref = refs[slots], refs[slots + 1]
        acc = dot(refs[0][...], w_ref[0], 1, 1)
        for s in range(1, slots):
            acc = acc + dot(refs[s][...], w_ref[s], 1, 1)
        out_ref[...] = narrow(acc)

    return pl.pallas_call(
        kernel,
        grid=(count // tile, width // cols),
        in_specs=[pl.BlockSpec((tile, both), lambda r, j: (start // tile + r, 0))] * slots
        + [pl.BlockSpec((slots, cols, both), lambda r, j: (0, j, 0))],
        out_specs=pl.BlockSpec((tile, cols), lambda r, j: (r, j)),
        out_shape=jax.ShapeDtypeStruct((count, width), BF16),
        compiler_params=pltpu.CompilerParams(vmem_limit_bytes=LIMIT),
        cost_estimate=cost(2 * count * width * slots * both, 2 * width * (count + slots * both)),
        name="rows_back",
    )(*d_pres, w_in)


def body(tokens, d_mixed, w_in, w_out, expert_ids, gate_fixed, placement):
    rows, width = tokens.shape
    slots = w_out.shape[0]
    ring, parts = lax.axis_size("expert"), lax.axis_size("dp")
    me_e, me_p = lax.axis_index("expert"), lax.axis_index("dp")
    pairs = ring_pairs(ring)
    top = expert_ids.shape[1]
    total = rows * ring

    meta = jnp.concatenate([expert_ids, gate_fixed // 256, gate_fixed % 256], axis=1)
    meta = jnp.pad(meta, ((0, 0), (0, 128 - 3 * top))).astype(BF16)
    x_blocks = ring_gather(jnp.concatenate([tokens, meta], axis=1), pairs)
    d_start, _ = lax.optimization_barrier((d_mixed, x_blocks[-3]))
    d_blocks = ring_gather(d_start, pairs)
    x = jnp.concatenate([b[:, :width] for b in x_blocks], axis=0)
    meta = jnp.concatenate([b[:, width:] for b in x_blocks], axis=0)
    d = jnp.concatenate(d_blocks, axis=0)

    local = me_e * slots + jnp.arange(slots, dtype=jnp.int32)
    names = jnp.arange(placement.shape[0], dtype=jnp.int32)
    held = jnp.sum(jnp.where(placement[None, :] == local[:, None], names[None, :], 0), axis=1)

    acts, lrs = zip(*[forward(x, meta, held, w_in, s, top) for s in range(slots)])
    mixed_part = mix(acts, w_out)

    core_pairs = [(i, i ^ 1) for i in range(parts)]
    chip_pairs = [(i, (i + parts // 2) % parts) for i in range(parts)]
    core, far, near = me_p % 2, (me_p // 2 + 1) % 2, me_p // 2
    order = jnp.stack([2 * far + 1 - core, 2 * near + 1 - core, 2 * far + core, 2 * near + core])

    d_pres, grads = [], []
    for s in range(slots):
        d_pre = backward(d, lrs[s], w_out, s)
        d_pres.append(d_pre)
        give_in, give_out, keep_in, keep_out = gradients(x, d, acts[s], d_pre, order, parts)
        pair = []
        for give, keep in ((give_in, keep_in), (give_out, keep_out)):
            got = lax.ppermute(give, "dp", core_pairs)
            away = lax.ppermute(narrow(wide(keep[0]) + wide(got[0])), "dp", chip_pairs)
            pair.append(narrow(wide(keep[1]) + wide(got[1]) + wide(away)))
        grads.append(pair)
    late = rows_back(d_pres, w_in, total // 2, total // 2)
    early = rows_back(d_pres, w_in, 0, total // 2)
    cut = lambda a: [a[i * rows : (i + 1) * rows] for i in range(a.shape[0] // rows)]
    mixed = ring_scatter(cut(mixed_part), pairs)
    d_tokens = ring_scatter(cut(early) + cut(late), pairs)
    return mixed, d_tokens, jnp.stack([g[0] for g in grads]), jnp.stack([g[1] for g in grads])


def solution(mesh):
    rows, slots = P(("dp", "expert"), None), P("expert", None, None)
    return jax.shard_map(
        body,
        mesh=mesh,
        in_specs=(rows, rows, slots, slots, rows, rows, P()),
        out_specs=(rows, rows, P("expert", "dp", None), P("expert", None, "dp")),
        check_vma=False,
    )
```

```python
import jax
import jax.numpy as jnp
from jax import lax
from jax.experimental import pallas as pl
from jax.experimental.pallas import tpu as pltpu
from jax.sharding import PartitionSpec as P


F32, BF16 = jnp.float32, jnp.bfloat16
LIMIT = 48 << 20
LANES = 128


def ring_pairs(count):
    order = list(range(0, count, 2)) + list(range(count - 1 - count % 2, 0, -2))
    ahead = [(order[i], order[(i + 1) % count]) for i in range(count)]
    return ahead, [(b, a) for a, b in ahead]


def narrow(a):
    return a.astype(BF16)


def wide(a):
    return a.astype(F32)


def dot(a, b, ca, cb):
    return lax.dot_general(a, b, (((ca,), (cb,)), ((), ())), preferred_element_type=F32)


def cost(flops, size):
    return pl.CostEstimate(flops=int(flops), bytes_accessed=int(size), transcendentals=0)


def call(kernel, flops, size, **kwargs):
    return pl.pallas_call(
        kernel, compiler_params=pltpu.CompilerParams(vmem_limit_bytes=LIMIT), cost_estimate=cost(flops, size), **kwargs
    )


def full(a):
    return pl.BlockSpec(a.shape, lambda *_: (0,) * a.ndim)


def route_rows(blocks, held, order, slots, room, lean, top, width, parts):
    flat = [part for block in blocks for part in block]
    sizes = [len(block) for block in blocks]
    count, rows = len(blocks), sum(part.shape[0] for part in blocks[0])
    part = width // parts

    def kernel(*refs):
        held_ref, order_ref, ins = refs[0], refs[1], list(refs[2 : 2 + len(flat)])
        outs, packed = refs[2 + len(flat) : -1], refs[-1]
        before = (
            lax.broadcasted_iota(jnp.int32, (rows, rows), 0)
            < lax.broadcasted_iota(jnp.int32, (rows, rows), 1)
        ).astype(BF16)
        place = lax.broadcasted_iota(jnp.int32, (room, rows), 0).astype(F32)
        kept = [[] for _ in range(slots)]
        for i, size in enumerate(sizes):
            pieces = [ins.pop(0)[...] for _ in range(size)]
            block = pieces[0] if size == 1 else jnp.concatenate(pieces, axis=0)
            meta = wide(block[:, width:]).T
            ids = meta[:top]
            fixed = meta[top : 2 * top] * 256.0 + meta[2 * top : 3 * top]
            gates = fixed / jnp.sum(fixed, axis=0, keepdims=True)
            rows_out, pick_out, gate_out = outs[3 * i : 3 * i + 3]
            picks = []
            for s in range(slots):
                same = ids == held_ref[s].astype(F32)
                hit = jnp.sum(jnp.where(same, 1.0, 0.0), axis=0, keepdims=True)
                gate = jnp.sum(jnp.where(same, gates, 0.0), axis=0, keepdims=True)
                rank = dot(narrow(jnp.broadcast_to(hit, (8, rows))), before, 1, 0)[:1]
                pick = jnp.where(place == rank, hit, 0.0)
                picks.append(pick)
                weight = jnp.sum(pick * gate, axis=1, keepdims=True)
                gate_out[s] = jnp.broadcast_to(weight, (room, LANES))
            pick = narrow(jnp.concatenate(picks, axis=0))
            pick_out[...] = pick
            sorted_rows = dot(pick, block[:, :width], 1, 0).reshape(slots, room, width)
            rows_out[...] = narrow(sorted_rows)
            for s in range(slots):
                kept[s].append(sorted_rows[s, :lean])
            if (i + 1) * lean % 16 == 0:
                n = len(kept[0]) * lean
                for s in range(slots):
                    packed[s, (i + 1) * lean - n : (i + 1) * lean, :] = narrow(jnp.concatenate(kept[s], axis=0))
                kept = [[] for _ in range(slots)]
        for j in range(parts):
            cols = pl.ds(pl.multiple_of(order_ref[j] * part, part), part)
            outs[3 * count + j][...] = packed[:, :, cols]

    shapes = [
        jax.ShapeDtypeStruct((slots, room, width), BF16),
        jax.ShapeDtypeStruct((slots * room, rows), BF16),
        jax.ShapeDtypeStruct((slots, room, LANES), F32),
    ] * count + [jax.ShapeDtypeStruct((slots, count * lean, part), BF16)] * parts
    outs = call(
        kernel,
        2 * count * slots * room * rows * width,
        2 * count * width * (rows + 2 * slots * room),
        in_specs=[pl.BlockSpec(memory_space=pltpu.SMEM)] * 2 + [full(a) for a in flat],
        out_specs=[full(a) for a in shapes],
        out_shape=shapes,
        scratch_shapes=[pltpu.VMEM((slots, count * lean, width), BF16)],
    )(held, order, *flat)
    return [outs[3 * i : 3 * i + 3] for i in range(count)], outs[3 * count :]


def pick_rows(blocks, picks, slots):
    flat = [part for block in blocks for part in block]
    sizes = [len(block) for block in blocks]
    count, width = len(blocks), flat[0].shape[1]
    total, rows = picks[0].shape

    def kernel(*refs):
        ins, sel, outs = list(refs[: len(flat)]), refs[len(flat) : len(flat) + count], refs[len(flat) + count :]
        for i, size in enumerate(sizes):
            parts = [ins.pop(0)[...] for _ in range(size)]
            block = parts[0] if size == 1 else jnp.concatenate(parts, axis=0)
            outs[i][...] = narrow(dot(sel[i][...], block, 1, 0)).reshape(slots, total // slots, width)

    shapes = [jax.ShapeDtypeStruct((slots, total // slots, width), BF16)] * count
    return call(
        kernel,
        2 * count * total * rows * width,
        2 * count * width * (rows + total),
        in_specs=[full(a) for a in flat + list(picks)],
        out_specs=[full(a) for a in shapes],
        out_shape=shapes,
    )(*flat, *picks)


def rows_of(refs):
    return jnp.concatenate([r[0] for r in refs], axis=0)


def forward(xs, gates, w_in, w_out, first, last):
    _, width, both = w_in.shape
    hidden, count, room = both // 2, len(xs), xs[0].shape[1]
    total, here = count * room, last - first

    def kernel(*refs):
        x_refs, g_refs = refs[:count], refs[count : 2 * count]
        wi_ref, wo_ref, out_ref, act_ref, lr_ref = refs[2 * count :]
        weight = rows_of(g_refs)[:, :1]
        pre = dot(rows_of(x_refs), wi_ref[0], 1, 0)
        gate, up = pre[:, :hidden], pre[:, hidden:]
        sig = jax.nn.sigmoid(gate)
        lean = weight * (gate * sig)
        act = narrow(lean * up)
        act_ref[0] = act
        lr_ref[0, :, :hidden] = weight * up * sig * (1.0 + gate * (1.0 - sig))
        lr_ref[0, :, hidden:] = lean
        out_ref[0] = narrow(dot(act, wo_ref[0], 1, 0)).reshape(count, room, width)

    at = lambda s: (s + first, 0, 0)
    shapes = [
        jax.ShapeDtypeStruct((here, count, room, width), BF16),
        jax.ShapeDtypeStruct((here, total, hidden), BF16),
        jax.ShapeDtypeStruct((here, total, both), F32),
    ]
    return call(
        kernel,
        2 * here * total * width * (both + hidden),
        2 * here * width * (2 * total + both + hidden),
        grid=(here,),
        in_specs=[pl.BlockSpec((1, room, width), at)] * count
        + [pl.BlockSpec((1, room, LANES), at)] * count
        + [pl.BlockSpec((1, width, both), at), pl.BlockSpec((1, hidden, width), at)],
        out_specs=[
            pl.BlockSpec((1, count, room, width), lambda s: (s, 0, 0, 0)),
            pl.BlockSpec((1, total, hidden), lambda s: (s, 0, 0)),
            pl.BlockSpec((1, total, both), lambda s: (s, 0, 0)),
        ],
        out_shape=shapes,
    )(*xs, *gates, w_in, w_out)


def backward(ds, lr, w_out, first, last, lean):
    count, (slots, room, width) = len(ds), ds[0].shape
    hidden, both = w_out.shape[1], lr.shape[2]
    total, here = count * room, last - first

    def kernel(*refs):
        d_refs = refs[:count]
        lr_ref, w_ref, all_ref, lean_ref = refs[count:]
        d_act = dot(rows_of(d_refs), w_ref[0], 1, 1)
        d_pre = jnp.concatenate([d_act * lr_ref[0, :, :hidden], d_act * lr_ref[0, :, hidden:]], axis=1)
        all_ref[0] = narrow(d_pre)
        rows = d_pre.reshape(count, room, both)[:, :lean].reshape(count * lean, both)
        lean_ref[0] = narrow(rows)

    at = lambda s: (s + first, 0, 0)
    return call(
        kernel,
        2 * here * total * width * hidden,
        2 * here * width * (total + hidden),
        grid=(here,),
        in_specs=[pl.BlockSpec((1, room, width), at)] * count
        + [pl.BlockSpec((1, total, both), lambda s: (s, 0, 0)), pl.BlockSpec((1, hidden, width), at)],
        out_specs=[
            pl.BlockSpec((1, total, both), lambda s: (s, 0, 0)),
            pl.BlockSpec((1, count * lean, both), lambda s: (s, 0, 0)),
        ],
        out_shape=[
            jax.ShapeDtypeStruct((here, total, both), BF16),
            jax.ShapeDtypeStruct((here, count * lean, both), BF16),
        ],
    )(*ds, lr, w_out)


def out_gradients(ds, acts, order, parts, first):
    count, (_, room, width) = len(ds), ds[0].shape
    here, total, hidden = acts.shape
    part, half = width // parts, parts // 2

    def kernel(*refs):
        order_ref, d_refs = refs[0], refs[1 : 1 + count]
        act_ref, first_ref, second_ref, whole = refs[1 + count :]
        whole[...] = narrow(dot(act_ref[0], rows_of(d_refs), 0, 0))
        for j in range(parts):
            cols = pl.ds(pl.multiple_of(order_ref[j] * part, part), part)
            (first_ref if j < half else second_ref)[j % half, 0] = whole[:, cols]

    shape = jax.ShapeDtypeStruct((half, here, hidden, part), BF16)
    spec = pl.BlockSpec((half, 1, hidden, part), lambda s, o: (0, s, 0, 0))
    return call(
        kernel,
        2 * here * total * width * hidden,
        2 * here * width * (total + hidden),
        grid_spec=pltpu.PrefetchScalarGridSpec(
            num_scalar_prefetch=1,
            grid=(here,),
            in_specs=[pl.BlockSpec((1, room, width), lambda s, o: (s + first, 0, 0))] * count
            + [pl.BlockSpec((1, total, hidden), lambda s, o: (s, 0, 0))],
            out_specs=[spec, spec],
            scratch_shapes=[pltpu.VMEM((hidden, width), BF16)],
        ),
        out_shape=[shape, shape],
    )(order, *ds, acts)


def in_gradients(xs, d_pres, first, last, into):
    slots, half_rows, part = xs[0].shape
    both, groups = d_pres[0].shape[2], len(d_pres)
    here = last - first

    def kernel(*refs):
        x = jnp.concatenate([r[0] for r in refs[: 2 * groups]], axis=0)
        d = jnp.concatenate([r[0] for r in refs[2 * groups : 3 * groups]], axis=0)
        refs[-1][0] = narrow(dot(x, d, 0, 0))

    at = lambda s: (s + first, 0, 0)
    return call(
        kernel,
        4 * here * groups * half_rows * part * both,
        4 * here * groups * half_rows * (part + both),
        grid=(here,),
        in_specs=[pl.BlockSpec((1, half_rows, part), at)] * (2 * groups)
        + [pl.BlockSpec((1, 2 * half_rows, both), lambda s: (s, 0, 0))] * groups
        + ([] if into is None else [pl.BlockSpec(memory_space=pl.ANY)]),
        out_specs=pl.BlockSpec((1, part, both), at),
        out_shape=jax.ShapeDtypeStruct((slots, part, both), BF16),
        input_output_aliases={} if into is None else {3 * groups: 0},
    )(*xs, *d_pres, *([] if into is None else [into]))


def rows_back(d_pres, w_in, count):
    slots, width, both = w_in.shape
    here, total = d_pres[0].shape[0], d_pres[0].shape[1]

    def kernel(*refs):
        w_ref, out_ref = refs[-2], refs[-1]
        for i in range(len(d_pres)):
            @pl.when(pl.program_id(0) // here == i)
            def _():
                out_ref[0] = narrow(dot(refs[i][0], w_ref[0], 1, 1)).reshape(out_ref.shape[1:])

    def at(i):
        return lambda s: (jnp.clip(s - i * here, 0, here - 1), 0, 0)

    return call(
        kernel,
        2 * total * width * slots * both,
        2 * width * slots * (total + both),
        grid=(slots,),
        in_specs=[pl.BlockSpec((1, total, both), at(i)) for i in range(len(d_pres))]
        + [pl.BlockSpec((1, width, both), lambda s: (s, 0, 0))],
        out_specs=pl.BlockSpec((1, count, total // count, width), lambda s: (s, 0, 0, 0)),
        out_shape=jax.ShapeDtypeStruct((slots, count, total // count, width), BF16),
    )(*d_pres, w_in)


def combine(outs, jobs, shapes):
    width = outs[0].shape[3]
    arrays, specs, plan = [], [], []
    for block, pick, addends in jobs:
        arrays += [o for o in outs] + [pick] + [a for _, a in addends]
        specs += [
            pl.BlockSpec((o.shape[0], 1, o.shape[2], width), lambda *_, b=block: (0, b, 0, 0)) for o in outs
        ]
        specs += [full(pick)] + [full(a) for _, a in addends]
        plan.append([at for at, _ in addends])
    out_shapes = [jax.ShapeDtypeStruct((n, width), BF16) for pieces in shapes for n in pieces]

    def kernel(*refs):
        ins, res = list(refs[: len(arrays)]), list(refs[len(arrays) :])
        for addends, pieces in zip(plan, shapes):
            rows = jnp.concatenate(
                [ins.pop(0)[...].reshape(-1, width) for _ in outs], axis=0
            )
            acc = dot(ins.pop(0)[...], rows, 0, 0)
            for at in addends:
                more = wide(ins.pop(0)[...])
                if more.shape[0] == acc.shape[0]:
                    acc = acc + more
                else:
                    cut = [acc[:at], acc[at : at + more.shape[0]] + more, acc[at + more.shape[0] :]]
                    acc = jnp.concatenate([c for c in cut if c.shape[0]], axis=0)
            at = 0
            for n in pieces:
                res.pop(0)[...] = narrow(acc[at : at + n])
                at += n

    size = sum(2 * a.size for a in out_shapes)
    return call(
        kernel,
        2 * len(jobs) * jobs[0][1].size * width,
        2 * len(jobs) * jobs[0][1].shape[0] * width + 3 * size,
        grid=(1,),
        in_specs=specs,
        out_specs=[full(a) for a in out_shapes],
        out_shape=out_shapes,
    )(*arrays)


def ring_scatter(outs, picks, pairs):
    ahead, back = pairs
    count, rows = len(ahead), picks[0].shape[1]
    half = rows // 2
    f, g = combine(outs, [(count - 1, picks[-1], [])], [[half, half]])
    offsets = (0, half)
    for step in range(count // 2 - 1, 0, -1):
        f = lax.ppermute(f, "expert", ahead)
        g = lax.ppermute(g, "expert", back)
        jobs = [(2 * step, picks[2 * step], [(offsets[0], f)]), (2 * step - 1, picks[2 * step - 1], [(offsets[1], g)])]
        f, g = combine(outs, jobs, [[rows], [rows]])
        offsets = (0, 0)
    f = lax.ppermute(f, "expert", ahead)
    g = lax.ppermute(g, "expert", back)
    return combine(outs, [(0, picks[0], [(0, f), (0, g)])], [[rows]])[0]


def ring_gather(block, pairs):
    ahead, back = pairs
    half = block.shape[0] // 2
    f = g = block
    blocks = [[block]]
    for _ in range(1, len(ahead) // 2):
        f = lax.ppermute(f, "expert", ahead)
        g = lax.ppermute(g, "expert", back)
        blocks += [[f], [g]]
    low = lax.ppermute(f[:half], "expert", ahead)
    high = lax.ppermute(g[half:], "expert", back)
    return blocks + [[low, high]], f


def body(tokens, d_mixed, w_in, w_out, expert_ids, gate_fixed, placement):
    rows, width = tokens.shape
    slots, experts, top = w_out.shape[0], placement.shape[0], expert_ids.shape[1]
    ring, parts = lax.axis_size("expert"), lax.axis_size("dp")
    me_e, me_p = lax.axis_index("expert"), lax.axis_index("dp")
    pairs = ring_pairs(ring)
    most = max(2, 5 * rows * top // (4 * experts))
    room, lean = -(-most // 16) * 16, -(-most // 8) * 8

    core_pairs = [(i, i ^ 1) for i in range(parts)]
    chip_pairs = [(i, (i + parts // 2) % parts) for i in range(parts)]
    far_pairs = [(i, (i ^ 1) + parts // 2 if i < parts // 2 else (i ^ 1) - parts // 2) for i in range(parts)]
    core, far, near = me_p % 2, (me_p // 2 + 1) % 2, me_p // 2
    order = jnp.stack([2 * far + 1 - core, 2 * near + 1 - core, 2 * far + core, 2 * near + core])
    routes = (far_pairs, core_pairs, chip_pairs)

    local = me_e * slots + jnp.arange(slots, dtype=jnp.int32)
    names = jnp.arange(experts, dtype=jnp.int32)
    held = jnp.sum(jnp.where(placement[None, :] == local[:, None], names[None, :], 0), axis=1)

    meta = jnp.concatenate([expert_ids, gate_fixed // 256, gate_fixed % 256], axis=1)
    meta = jnp.pad(meta, ((0, 0), (0, LANES - 3 * top))).astype(BF16)
    x_blocks, last = ring_gather(jnp.concatenate([tokens, meta], axis=1), pairs)
    start, _ = lax.optimization_barrier((d_mixed, last))
    d_blocks, _ = ring_gather(start, pairs)

    half = ring // 2
    routed, columns = [], []
    for i in range(2):
        got, cols = route_rows(x_blocks[i * half : (i + 1) * half], held, order, slots, room, lean, top, width, parts)
        routed += got
        columns.append([lax.ppermute(cols[j], "dp", routes[j]) for j in range(parts - 1)] + [cols[-1]])
    xs, picks, gates = (list(a) for a in zip(*routed))

    pair = slots // 2
    lows = range(0, slots, pair)
    outs, acts, lrs = zip(*[forward(xs, gates, w_in, w_out, low, low + pair) for low in lows])
    ds = []
    for low, high in ((0, half), (half, ring - 1), (ring - 1, ring)):
        ds += pick_rows(d_blocks[low:high], picks[low:high], slots)

    d_pres, leans, grads = [], [], []
    for low, act, lr in zip(lows, acts, lrs):
        d_pre, mine = backward(ds, lr, w_out, low, low + pair, lean)
        d_pres.append(d_pre)
        across = lax.ppermute(mine, "dp", chip_pairs)
        beside = lax.ppermute(mine, "dp", core_pairs)
        both = lax.ppermute(across, "dp", core_pairs)
        leans.append([both, beside, across, mine])
        give, keep = out_gradients(ds, act, order, parts, low)
        got = lax.ppermute(give, "dp", core_pairs)
        away = lax.ppermute(narrow(wide(keep[0]) + wide(got[0])), "dp", chip_pairs)
        grads.append(narrow(wide(keep[1]) + wide(got[1]) + wide(away)))
    grad_out = jnp.concatenate(grads, axis=0)
    rows_by_group = [columns[i][j] for j in range(parts) for i in range(2)]
    grad_in = None
    for low, d_lean in zip(lows, leans):
        grad_in = in_gradients(rows_by_group, d_lean, low, low + pair, grad_in)

    mixed = ring_scatter(outs, picks, pairs)
    backs = rows_back(d_pres, w_in, ring)
    d_tokens = ring_scatter([backs], picks, pairs)
    return mixed, d_tokens, grad_in, grad_out


def solution(mesh):
    rows, slots = P(("dp", "expert"), None), P("expert", None, None)
    return jax.shard_map(
        body,
        mesh=mesh,
        in_specs=(rows, rows, slots, slots, rows, rows, P()),
        out_specs=(rows, rows, P("expert", "dp", None), P("expert", None, "dp")),
        check_vma=False,
    )
```

```python
import jax
import jax.numpy as jnp
from jax import lax
from jax.experimental import pallas as pl
from jax.experimental.pallas import tpu as pltpu
from jax.sharding import PartitionSpec as P


F32, BF16 = jnp.float32, jnp.bfloat16
LIMIT = 20 << 20
LANES = 128


def ring_pairs(count):
    order = list(range(0, count, 2)) + list(range(count - 1 - count % 2, 0, -2))
    ahead = [(order[i], order[(i + 1) % count]) for i in range(count)]
    return ahead, [(b, a) for a, b in ahead]


def in_hbm(a):
    return pltpu.with_memory_space_constraint(a, pltpu.HBM)


def narrow(a):
    return a.astype(BF16)


def wide(a):
    return a.astype(F32)


def dot(a, b, ca, cb):
    return lax.dot_general(a, b, (((ca,), (cb,)), ((), ())), preferred_element_type=F32)


def cost(flops, size):
    return pl.CostEstimate(flops=int(flops), bytes_accessed=int(size), transcendentals=0)


def call(kernel, flops, size, **kwargs):
    return pl.pallas_call(
        kernel, compiler_params=pltpu.CompilerParams(vmem_limit_bytes=LIMIT), cost_estimate=cost(flops, size), **kwargs
    )


def full(a):
    return pl.BlockSpec(a.shape, lambda *_: (0,) * a.ndim)


def pack_rows(tokens, expert_ids, gate_fixed):
    rows, width = tokens.shape
    top, half = expert_ids.shape[1], rows // 2
    expert_ids, gate_fixed = expert_ids.T, gate_fixed.T

    def kernel(x_ref, ids_ref, gate_ref, low_ref, high_ref):
        lane = lax.broadcasted_iota(jnp.int32, (top, LANES), 1)
        here = lax.broadcasted_iota(jnp.int32, (top, LANES), 0)
        gate = gate_ref[...]
        meta = jnp.zeros((rows, LANES), F32)
        for i, a in enumerate((ids_ref[...], lax.shift_right_logical(gate, 8), gate & 255)):
            spread = jnp.where(lane == here + i * top, 1.0, 0.0)
            meta = meta + dot(narrow(wide(a)), narrow(spread), 0, 0)
        for i, ref in enumerate((low_ref, high_ref)):
            ref[:, :width] = x_ref[i * half : (i + 1) * half, :]
            ref[:, width:] = narrow(meta[i * half : (i + 1) * half])

    shape = jax.ShapeDtypeStruct((half, width + LANES), BF16)
    return call(
        kernel,
        2 * rows * LANES * top,
        4 * rows * width,
        in_specs=[full(tokens), full(expert_ids), full(gate_fixed)],
        out_specs=[full(shape)] * 2,
        out_shape=[shape] * 2,
    )(tokens, expert_ids, gate_fixed)


def route_rows(blocks, placement, info, slots, room, lean, top, width, parts):
    flat = [part for block in blocks for part in block]
    sizes = [len(block) for block in blocks]
    count, rows = len(blocks), sum(part.shape[0] for part in blocks[0])
    part = width // parts

    def kernel(*refs):
        place_ref, info_ref, ins = refs[0], refs[1], list(refs[2 : 2 + len(flat)])
        outs, packed = refs[2 + len(flat) : -1], refs[-1]
        before = (
            lax.broadcasted_iota(jnp.int32, (rows, rows), 0)
            < lax.broadcasted_iota(jnp.int32, (rows, rows), 1)
        ).astype(BF16)
        place = lax.broadcasted_iota(jnp.int32, (room, rows), 0).astype(F32)
        kept = [[] for _ in range(slots)]
        held = [jnp.int32(0)] * slots
        for e in range(placement.shape[0]):
            for s in range(slots):
                held[s] = jnp.where(place_ref[e] == info_ref[parts] + s, e, held[s])
        for i, size in enumerate(sizes):
            pieces = [ins.pop(0)[...] for _ in range(size)]
            block = pieces[0] if size == 1 else jnp.concatenate(pieces, axis=0)
            meta = wide(block[:, width:]).T
            ids = meta[:top]
            fixed = meta[top : 2 * top] * 256.0 + meta[2 * top : 3 * top]
            gates = fixed / jnp.sum(fixed, axis=0, keepdims=True)
            rows_out, pick_out, gate_out = outs[3 * i : 3 * i + 3]
            picks = []
            for s in range(slots):
                same = ids == held[s].astype(F32)
                hit = jnp.sum(jnp.where(same, 1.0, 0.0), axis=0, keepdims=True)
                gate = jnp.sum(jnp.where(same, gates, 0.0), axis=0, keepdims=True)
                rank = dot(narrow(jnp.broadcast_to(hit, (8, rows))), before, 1, 0)[:1]
                pick = jnp.where(place == rank, hit, 0.0)
                picks.append(pick)
                weight = jnp.sum(pick * gate, axis=1, keepdims=True)
                gate_out[s] = jnp.broadcast_to(weight, (room, LANES))
            pick = narrow(jnp.concatenate(picks, axis=0))
            pick_out[...] = pick
            sorted_rows = dot(pick, block[:, :width], 1, 0).reshape(slots, room, width)
            rows_out[...] = narrow(sorted_rows)
            for s in range(slots):
                kept[s].append(sorted_rows[s, :lean])
            if (i + 1) * lean % 16 == 0:
                n = len(kept[0]) * lean
                for s in range(slots):
                    packed[s, (i + 1) * lean - n : (i + 1) * lean, :] = narrow(jnp.concatenate(kept[s], axis=0))
                kept = [[] for _ in range(slots)]
        for j in range(parts):
            cols = pl.ds(pl.multiple_of(info_ref[j] * part, part), part)
            outs[3 * count + j][...] = packed[:, :, cols]

    shapes = [
        jax.ShapeDtypeStruct((slots, room, width), BF16),
        jax.ShapeDtypeStruct((slots * room, rows), BF16),
        jax.ShapeDtypeStruct((slots, room, LANES), F32),
    ] * count + [jax.ShapeDtypeStruct((slots, count * lean, part), BF16)] * parts
    outs = call(
        kernel,
        2 * count * slots * room * rows * width,
        2 * count * width * (rows + 2 * slots * room),
        in_specs=[pl.BlockSpec(memory_space=pltpu.SMEM)] * 2 + [full(a) for a in flat],
        out_specs=[full(a) for a in shapes],
        out_shape=shapes,
        scratch_shapes=[pltpu.VMEM((slots, count * lean, width), BF16)],
    )(placement, info, *flat)
    return [outs[3 * i : 3 * i + 3] for i in range(count)], outs[3 * count :]


def pick_rows(blocks, picks, slots):
    flat = [part for block in blocks for part in block]
    sizes = [len(block) for block in blocks]
    count, width = len(blocks), flat[0].shape[1]
    total, rows = picks[0].shape

    def kernel(*refs):
        ins, sel, outs = list(refs[: len(flat)]), refs[len(flat) : len(flat) + count], refs[len(flat) + count :]
        for i, size in enumerate(sizes):
            parts = [ins.pop(0)[...] for _ in range(size)]
            block = parts[0] if size == 1 else jnp.concatenate(parts, axis=0)
            outs[i][...] = narrow(dot(sel[i][...], block, 1, 0)).reshape(slots, total // slots, width)

    shapes = [jax.ShapeDtypeStruct((slots, total // slots, width), BF16)] * count
    return call(
        kernel,
        2 * count * total * rows * width,
        2 * count * width * (rows + total),
        in_specs=[full(a) for a in flat + list(picks)],
        out_specs=[full(a) for a in shapes],
        out_shape=shapes,
    )(*flat, *picks)


def rows_of(refs):
    return jnp.concatenate([r[0] for r in refs], axis=0)


def forward(xs, gates, w_in, w_out):
    slots, width, both = w_in.shape
    hidden, count, room = both // 2, len(xs), xs[0].shape[1]
    total = count * room

    def kernel(*refs):
        x_refs, g_refs = refs[:count], refs[count : 2 * count]
        wi_ref, wo_ref, out_ref, act_ref, lr_ref = refs[2 * count :]
        weight = rows_of(g_refs)[:, :1]
        pre = dot(rows_of(x_refs), wi_ref[0], 1, 0)
        gate, up = pre[:, :hidden], pre[:, hidden:]
        sig = jax.nn.sigmoid(gate)
        lean = weight * (gate * sig)
        act = narrow(lean * up)
        act_ref[0] = act
        lr_ref[0, :, :hidden] = weight * up * sig * (1.0 + gate * (1.0 - sig))
        lr_ref[0, :, hidden:] = lean
        out_ref[0] = narrow(dot(act, wo_ref[0], 1, 0)).reshape(count, room, width)

    at = lambda s: (s, 0, 0)
    shapes = [
        jax.ShapeDtypeStruct((slots, count, room, width), BF16),
        jax.ShapeDtypeStruct((slots, total, hidden), BF16),
        jax.ShapeDtypeStruct((slots, total, both), F32),
    ]
    return call(
        kernel,
        2 * slots * total * width * (both + hidden),
        2 * slots * width * (2 * total + both + hidden),
        grid=(slots,),
        in_specs=[pl.BlockSpec((1, room, width), at)] * count
        + [pl.BlockSpec((1, room, LANES), at)] * count
        + [pl.BlockSpec((1, width, both), at), pl.BlockSpec((1, hidden, width), at)],
        out_specs=[
            pl.BlockSpec((1, count, room, width), lambda s: (s, 0, 0, 0)),
            pl.BlockSpec((1, total, hidden), at),
            pl.BlockSpec((1, total, both), at),
        ],
        out_shape=shapes,
    )(*xs, *gates, w_in, w_out)


def backward(ds, lrs, w_out, first, last, lean):
    count, (slots, room, width) = len(ds), ds[0].shape
    hidden, both = w_out.shape[1], lrs[0].shape[2]
    total, here = count * room, last - first

    def kernel(*refs):
        d_refs = refs[:count]
        w_ref, all_ref, lean_ref = refs[count + len(lrs) :]
        d_act = dot(rows_of(d_refs), w_ref[0], 1, 1)
        lr = rows_of(refs[count : count + len(lrs)])
        d_pre = jnp.concatenate([d_act * lr[:, :hidden], d_act * lr[:, hidden:]], axis=1)
        all_ref[0] = narrow(d_pre)
        rows = d_pre.reshape(count, room, both)[:, :lean].reshape(count * lean, both)
        lean_ref[0] = narrow(rows)

    at = lambda s: (s + first, 0, 0)
    return call(
        kernel,
        2 * here * total * width * hidden,
        2 * here * width * (total + hidden),
        grid=(here,),
        in_specs=[pl.BlockSpec((1, room, width), at)] * count
        + [pl.BlockSpec((1, total // len(lrs), both), at)] * len(lrs)
        + [pl.BlockSpec((1, hidden, width), at)],
        out_specs=[
            pl.BlockSpec((1, total, both), lambda s: (s, 0, 0)),
            pl.BlockSpec((1, count * lean, both), lambda s: (s, 0, 0)),
        ],
        out_shape=[
            jax.ShapeDtypeStruct((here, total, both), BF16),
            jax.ShapeDtypeStruct((here, count * lean, both), BF16),
        ],
    )(*ds, *lrs, w_out)


def out_gradients(ds, acts, order, parts, first, here):
    count, (_, room, width) = len(ds), ds[0].shape
    total, hidden = count * room, acts[0].shape[2]
    part, half = width // parts, parts // 2

    def kernel(*refs):
        order_ref, d_refs = refs[0], refs[1 : 1 + count]
        act_refs, (first_ref, second_ref, whole) = refs[1 + count : -3], refs[-3:]
        whole[...] = narrow(dot(rows_of(act_refs), rows_of(d_refs), 0, 0))
        for j in range(parts):
            cols = pl.ds(pl.multiple_of(order_ref[j] * part, part), part)
            (first_ref if j < half else second_ref)[j % half, 0] = whole[:, cols]

    shape = jax.ShapeDtypeStruct((half, here, hidden, part), BF16)
    spec = pl.BlockSpec((half, 1, hidden, part), lambda s, o: (0, s, 0, 0))
    return call(
        kernel,
        2 * here * total * width * hidden,
        2 * here * width * (total + hidden),
        grid_spec=pltpu.PrefetchScalarGridSpec(
            num_scalar_prefetch=1,
            grid=(here,),
            in_specs=[pl.BlockSpec((1, room, width), lambda s, o: (s + first, 0, 0))] * count
            + [pl.BlockSpec((1, total // len(acts), hidden), lambda s, o: (s + first, 0, 0))] * len(acts),
            out_specs=[spec, spec],
            scratch_shapes=[pltpu.VMEM((hidden, width), BF16)],
        ),
        out_shape=[shape, shape],
    )(order, *ds, *acts)


def finish(pieces):
    arrays = [a for piece in pieces for a in piece]
    here, hidden, part = pieces[0][2].shape
    shape = jax.ShapeDtypeStruct((here * len(pieces), hidden, part), BF16)

    def kernel(*refs):
        for i in range(len(pieces)):
            keep, got, away = refs[3 * i : 3 * i + 3]
            refs[-1][i * here : (i + 1) * here] = narrow(wide(keep[0]) + wide(got[0]) + wide(away[...]))

    own = pl.BlockSpec((1, here, hidden, part), lambda *_: (1, 0, 0, 0))
    return call(
        kernel,
        3 * here * hidden * part,
        8 * here * hidden * part,
        grid=(1,),
        in_specs=[own, own, full(pieces[0][2])] * len(pieces),
        out_specs=full(shape),
        out_shape=shape,
    )(*arrays)


def in_gradients(xs, d_pres, first, last, into):
    slots, half_rows, part = xs[0].shape
    both, groups = d_pres[0].shape[2], len(d_pres)
    here = last - first

    def kernel(*refs):
        x = jnp.concatenate([r[0] for r in refs[: 2 * groups]], axis=0)
        d = jnp.concatenate([r[0] for r in refs[2 * groups : 3 * groups]], axis=0)
        refs[-1][0] = narrow(dot(x, d, 0, 0))

    at = lambda s: (s + first, 0, 0)
    return call(
        kernel,
        4 * here * groups * half_rows * part * both,
        4 * here * groups * half_rows * (part + both),
        grid=(here,),
        in_specs=[pl.BlockSpec((1, half_rows, part), at)] * (2 * groups)
        + [pl.BlockSpec((1, 2 * half_rows, both), lambda s: (s, 0, 0))] * groups
        + ([] if into is None else [pl.BlockSpec(memory_space=pl.ANY)]),
        out_specs=pl.BlockSpec((1, part, both), at),
        out_shape=jax.ShapeDtypeStruct((slots, part, both), BF16),
        input_output_aliases={} if into is None else {3 * groups: 0},
    )(*xs, *d_pres, *([] if into is None else [into]))


def rows_back(d_pre, w_in, count, first):
    here, total, both = d_pre.shape
    width = w_in.shape[1]

    def kernel(d_ref, w_ref, out_ref):
        out_ref[0] = narrow(dot(d_ref[0], w_ref[0], 1, 1)).reshape(out_ref.shape[1:])

    return call(
        kernel,
        2 * total * width * here * both,
        2 * width * here * (total + both),
        grid=(here,),
        in_specs=[
            pl.BlockSpec((1, total, both), lambda s: (s, 0, 0)),
            pl.BlockSpec((1, width, both), lambda s: (s + first, 0, 0)),
        ],
        out_specs=pl.BlockSpec((1, count, total // count, width), lambda s: (s, 0, 0, 0)),
        out_shape=jax.ShapeDtypeStruct((here, count, total // count, width), BF16),
    )(d_pre, w_in)


def combine(outs, jobs, shapes):
    width = outs[0][0].shape[3]
    arrays, specs, plan = [], [], []
    for block, pick, addends in jobs:
        count = outs[0][0].shape[1]
        here, block = outs[block // count], block % count
        arrays += [o for o in here] + [pick] + [a for _, a in addends]
        specs += [
            pl.BlockSpec((o.shape[0], 1, o.shape[2], width), lambda *_, b=block: (0, b, 0, 0)) for o in here
        ]
        specs += [full(pick)] + [full(a) for _, a in addends]
        plan.append([at for at, _ in addends])
    out_shapes = [jax.ShapeDtypeStruct((n, width), BF16) for pieces in shapes for _, n in pieces]

    def kernel(*refs):
        ins, res = list(refs[: len(arrays)]), list(refs[len(arrays) :])
        for addends, pieces in zip(plan, shapes):
            rows = jnp.concatenate(
                [ins.pop(0)[...].reshape(-1, width) for _ in outs[0]], axis=0
            )
            acc = dot(ins.pop(0)[...], rows, 0, 0)
            for at in addends:
                more = wide(ins.pop(0)[...])
                if more.shape[0] == acc.shape[0]:
                    acc = acc + more
                else:
                    cut = [acc[:at], acc[at : at + more.shape[0]] + more, acc[at + more.shape[0] :]]
                    acc = jnp.concatenate([c for c in cut if c.shape[0]], axis=0)
            for at, n in pieces:
                res.pop(0)[...] = narrow(acc[at : at + n])

    size = sum(2 * a.size for a in out_shapes)
    return call(
        kernel,
        2 * len(jobs) * jobs[0][1].size * width,
        2 * len(jobs) * jobs[0][1].shape[0] * width + 3 * size,
        grid=(1,),
        in_specs=specs,
        out_specs=[full(a) for a in out_shapes],
        out_shape=out_shapes,
    )(*arrays)


def ring_scatter(outs, picks, pairs):
    ahead, back = pairs
    count, rows = len(ahead), picks[0].shape[1]
    half = rows // 2
    f, g = combine(outs, [(count - 1, picks[-1], [])], [[(0, half), (half, half)]])
    offsets = (0, half)
    for step in range(count // 2 - 1, 0, -1):
        f = lax.ppermute(f, "expert", ahead)
        g = lax.ppermute(g, "expert", back)
        jobs = [(2 * step, picks[2 * step], [(offsets[0], f)]), (2 * step - 1, picks[2 * step - 1], [(offsets[1], g)])]
        f, g = combine(outs, jobs, [[(0, rows)], [(0, rows)]])
        offsets = (0, 0)
    f = lax.ppermute(f, "expert", ahead)
    g = lax.ppermute(g, "expert", back)
    return combine(outs, [(0, picks[0], [(0, f), (0, g)])], [[(0, rows)]])[0]


def ring_scatter_halves(outs, picks, pairs):
    ahead, back = pairs
    count, rows = len(ahead), picks[0].shape[1]
    half, last = rows // 2, len(ahead) // 2
    lows, highs = (0, half), (half, half)
    lf, hg = combine(outs, [(count - 1, picks[-1], [])], [[lows, highs]])
    lg = hf = None
    for stage in range(1, last + 1):
        lf = lax.ppermute(lf, "expert", ahead)
        lg = None if lg is None else lax.ppermute(lg, "expert", back)
        hf = None if hf is None else lax.ppermute(hf, "expert", ahead)
        hg = lax.ppermute(hg, "expert", back)
        if stage == last:
            break
        fwd, bwd = 2 * (last - stage), 2 * (last - stage) - 1
        jobs = lambda at, f, g: [
            (b, picks[b], [] if a is None else [(at, a)]) for b, a in ((fwd, f), (bwd, g))
        ]
        lf, lg = combine(outs, jobs(0, lf, lg), [[lows], [lows]])
        hf, hg = combine(outs, jobs(half, hf, hg), [[highs], [highs]])
    addends = [(0, lf), (0, lg), (half, hf), (half, hg)]
    return combine(outs, [(0, picks[0], addends)], [[(0, rows)]])[0]


def ring_gather(block, pairs):
    ahead, back = pairs
    half = block.shape[0] // 2
    f = g = block
    blocks = [[block]]
    for _ in range(1, len(ahead) // 2):
        f = lax.ppermute(f, "expert", ahead)
        g = lax.ppermute(g, "expert", back)
        blocks += [[f], [g]]
    low = lax.ppermute(f[:half], "expert", ahead)
    high = lax.ppermute(g[half:], "expert", back)
    return blocks + [[low, high]]


def ring_gather_halves(low, high, pairs):
    ahead, back = pairs
    lf = lg = low
    hf = hg = high
    blocks = [[low, high]]
    for _ in range(1, len(ahead) // 2):
        lf = lax.ppermute(lf, "expert", ahead)
        lg = lax.ppermute(lg, "expert", back)
        hf = lax.ppermute(hf, "expert", ahead)
        hg = lax.ppermute(hg, "expert", back)
        blocks += [[lf, hf], [lg, hg]]
    low = lax.ppermute(lf, "expert", ahead)
    high = lax.ppermute(hg, "expert", back)
    return blocks + [[low, high]]


def body(tokens, d_mixed, w_in, w_out, expert_ids, gate_fixed, placement):
    rows, width = tokens.shape
    slots, experts, top = w_out.shape[0], placement.shape[0], expert_ids.shape[1]
    ring, parts = lax.axis_size("expert"), lax.axis_size("dp")
    me_e, me_p = lax.axis_index("expert"), lax.axis_index("dp")
    pairs = ring_pairs(ring)
    most = max(2, 5 * rows * top // (4 * experts))
    room, lean = -(-most // 16) * 16, -(-most // 8) * 8

    core_pairs = [(i, i ^ 1) for i in range(parts)]
    chip_pairs = [(i, (i + parts // 2) % parts) for i in range(parts)]
    far_pairs = [(i, (i ^ 1) + parts // 2 if i < parts // 2 else (i ^ 1) - parts // 2) for i in range(parts)]
    core, far, near = me_p % 2, (me_p // 2 + 1) % 2, me_p // 2
    order = jnp.stack([2 * far + 1 - core, 2 * near + 1 - core, 2 * far + core, 2 * near + core])
    routes = (far_pairs, core_pairs, chip_pairs)

    info = jnp.concatenate([order, (me_e * slots)[None]])
    w_in, w_out = in_hbm(w_in), in_hbm(w_out)
    x_blocks = ring_gather_halves(*pack_rows(tokens, expert_ids, gate_fixed), pairs)
    d_blocks = ring_gather(d_mixed, pairs)

    x_blocks = [[in_hbm(a) for a in block] for block in x_blocks]
    half = ring // 2
    routed, columns = [], []
    for i in range(2):
        got, cols = route_rows(
            x_blocks[i * half : (i + 1) * half], placement, info, slots, room, lean, top, width, parts
        )
        routed += got
        columns.append([lax.ppermute(cols[j], "dp", routes[j]) for j in range(parts - 1)] + [cols[-1]])
    xs, picks, gates = (list(a) for a in zip(*routed))

    pair = slots // 2
    lows = range(0, slots, pair)
    outs, acts, lrs = zip(
        *[forward(xs[i * half : (i + 1) * half], gates[i * half : (i + 1) * half], w_in, w_out) for i in range(2)]
    )
    ds = []
    for low, high in ((0, half), (half, ring - 1), (ring - 1, ring)):
        ds += pick_rows(d_blocks[low:high], picks[low:high], slots)

    d_pres, leans, grads = [], [], []
    for low in lows:
        d_pre, mine = backward(ds, lrs, w_out, low, low + pair, lean)
        d_pres.append(d_pre)
        across = lax.ppermute(mine, "dp", chip_pairs)
        beside = lax.ppermute(mine, "dp", core_pairs)
        both = lax.ppermute(across, "dp", core_pairs)
        leans.append([both, beside, across, mine])
        give, keep = out_gradients(ds, acts, order, parts, low, pair)
        got = lax.ppermute(give, "dp", core_pairs)
        away = lax.ppermute(narrow(wide(keep[0]) + wide(got[0])), "dp", chip_pairs)
        grads.append((keep, got, away))
    grad_out = finish(grads)
    rows_by_group = [columns[i][j] for j in range(parts) for i in range(2)]
    grad_in = None
    for low, d_lean in zip(lows, leans):
        grad_in = in_gradients(rows_by_group, d_lean, low, low + pair, grad_in)

    mixed = ring_scatter([[o] for o in outs], picks, pairs)
    backs = [rows_back(d_pre, w_in, ring, low) for low, d_pre in zip(lows, d_pres)]
    d_tokens = ring_scatter_halves([backs], picks, pairs)
    return mixed, d_tokens, grad_in, grad_out


def solution(mesh):
    rows, slots = P(("dp", "expert"), None), P("expert", None, None)
    return jax.shard_map(
        body,
        mesh=mesh,
        in_specs=(rows, rows, slots, slots, rows, rows, P()),
        out_specs=(rows, rows, P("expert", "dp", None), P("expert", None, "dp")),
        check_vma=False,
    )
```

```python
import jax
import jax.numpy as jnp
from jax import lax
from jax.experimental import pallas as pl
from jax.experimental.pallas import tpu as pltpu
from jax.sharding import PartitionSpec as P


F32, BF16 = jnp.float32, jnp.bfloat16
LIMIT = 20 << 20
LANES = 128


def ring_pairs(count):
    order = list(range(0, count, 2)) + list(range(count - 1 - count % 2, 0, -2))
    ahead = [(order[i], order[(i + 1) % count]) for i in range(count)]
    return ahead, [(b, a) for a, b in ahead]


def in_hbm(a):
    return pltpu.with_memory_space_constraint(a, pltpu.HBM)


def narrow(a):
    return a.astype(BF16)


def wide(a):
    return a.astype(F32)


def dot(a, b, ca, cb):
    return lax.dot_general(a, b, (((ca,), (cb,)), ((), ())), preferred_element_type=F32)


def cost(flops, size):
    return pl.CostEstimate(flops=int(flops), bytes_accessed=int(size), transcendentals=0)


def call(kernel, flops, size, **kwargs):
    return pl.pallas_call(
        kernel, compiler_params=pltpu.CompilerParams(vmem_limit_bytes=LIMIT), cost_estimate=cost(flops, size), **kwargs
    )


def full(a):
    return pl.BlockSpec(a.shape, lambda *_: (0,) * a.ndim)


def pack_rows(tokens, expert_ids, gate_fixed):
    rows, width = tokens.shape
    top, half = expert_ids.shape[1], rows // 2
    tokens, expert_ids, gate_fixed = in_hbm(tokens), in_hbm(expert_ids.T), in_hbm(gate_fixed.T)

    def kernel(x_ref, ids_ref, gate_ref, low_ref, high_ref):
        lane = lax.broadcasted_iota(jnp.int32, (top, LANES), 1)
        here = lax.broadcasted_iota(jnp.int32, (top, LANES), 0)
        gate = gate_ref[...]
        meta = jnp.zeros((rows, LANES), F32)
        for i, a in enumerate((ids_ref[...], lax.shift_right_logical(gate, 8), gate & 255)):
            spread = jnp.where(lane == here + i * top, 1.0, 0.0)
            meta = meta + dot(narrow(wide(a)), narrow(spread), 0, 0)
        for i, ref in enumerate((low_ref, high_ref)):
            ref[:, :width] = x_ref[i * half : (i + 1) * half, :]
            ref[:, width:] = narrow(meta[i * half : (i + 1) * half])

    shape = jax.ShapeDtypeStruct((half, width + LANES), BF16)
    return call(
        kernel,
        2 * rows * LANES * top,
        4 * rows * width,
        in_specs=[full(tokens), full(expert_ids), full(gate_fixed)],
        out_specs=[full(shape)] * 2,
        out_shape=[shape] * 2,
    )(tokens, expert_ids, gate_fixed)


def route_rows(blocks, placement, info, slots, room, lean, top, width, parts):
    flat = [part for block in blocks for part in block]
    sizes = [len(block) for block in blocks]
    count, rows = len(blocks), sum(part.shape[0] for part in blocks[0])
    part = width // parts

    def kernel(*refs):
        place_ref, info_ref, ins = refs[0], refs[1], list(refs[2 : 2 + len(flat)])
        outs, packed = refs[2 + len(flat) : -1], refs[-1]
        before = (
            lax.broadcasted_iota(jnp.int32, (rows, rows), 0)
            < lax.broadcasted_iota(jnp.int32, (rows, rows), 1)
        ).astype(BF16)
        place = lax.broadcasted_iota(jnp.int32, (room, rows), 0).astype(F32)
        kept = [[] for _ in range(slots)]
        held = [jnp.int32(0)] * slots
        for e in range(placement.shape[0]):
            for s in range(slots):
                held[s] = jnp.where(place_ref[e] == info_ref[parts] + s, e, held[s])
        for i, size in enumerate(sizes):
            pieces = [ins.pop(0)[...] for _ in range(size)]
            block = pieces[0] if size == 1 else jnp.concatenate(pieces, axis=0)
            meta = wide(block[:, width:]).T
            ids = meta[:top]
            fixed = meta[top : 2 * top] * 256.0 + meta[2 * top : 3 * top]
            gates = fixed / jnp.sum(fixed, axis=0, keepdims=True)
            rows_out, pick_out, gate_out = outs[3 * i : 3 * i + 3]
            picks = []
            for s in range(slots):
                same = ids == held[s].astype(F32)
                hit = jnp.sum(jnp.where(same, 1.0, 0.0), axis=0, keepdims=True)
                gate = jnp.sum(jnp.where(same, gates, 0.0), axis=0, keepdims=True)
                rank = dot(narrow(jnp.broadcast_to(hit, (8, rows))), before, 1, 0)[:1]
                pick = jnp.where(place == rank, hit, 0.0)
                picks.append(pick)
                weight = jnp.sum(pick * gate, axis=1, keepdims=True)
                gate_out[s] = jnp.broadcast_to(weight, (room, LANES))
            pick = narrow(jnp.concatenate(picks, axis=0))
            pick_out[...] = pick
            sorted_rows = dot(pick, block[:, :width], 1, 0).reshape(slots, room, width)
            rows_out[...] = narrow(sorted_rows)
            for s in range(slots):
                kept[s].append(sorted_rows[s, :lean])
            if (i + 1) * lean % 16 == 0:
                n = len(kept[0]) * lean
                for s in range(slots):
                    packed[s, (i + 1) * lean - n : (i + 1) * lean, :] = narrow(jnp.concatenate(kept[s], axis=0))
                kept = [[] for _ in range(slots)]
        for j in range(parts):
            cols = pl.ds(pl.multiple_of(info_ref[j] * part, part), part)
            outs[3 * count + j][...] = packed[:, :, cols]

    shapes = [
        jax.ShapeDtypeStruct((slots, room, width), BF16),
        jax.ShapeDtypeStruct((slots * room, rows), BF16),
        jax.ShapeDtypeStruct((slots, room, LANES), F32),
    ] * count + [jax.ShapeDtypeStruct((slots, count * lean, part), BF16)] * parts
    outs = call(
        kernel,
        2 * count * slots * room * rows * width,
        2 * count * width * (rows + 2 * slots * room),
        in_specs=[pl.BlockSpec(memory_space=pltpu.SMEM)] * 2 + [full(a) for a in flat],
        out_specs=[full(a) for a in shapes],
        out_shape=shapes,
        scratch_shapes=[pltpu.VMEM((slots, count * lean, width), BF16)],
    )(placement, info, *flat)
    return [outs[3 * i : 3 * i + 3] for i in range(count)], outs[3 * count :]


def pick_rows(blocks, picks, slots):
    flat = [part for block in blocks for part in block]
    sizes = [len(block) for block in blocks]
    count, width = len(blocks), flat[0].shape[1]
    total, rows = picks[0].shape

    def kernel(*refs):
        ins, sel, outs = list(refs[: len(flat)]), refs[len(flat) : len(flat) + count], refs[len(flat) + count :]
        for i, size in enumerate(sizes):
            parts = [ins.pop(0)[...] for _ in range(size)]
            block = parts[0] if size == 1 else jnp.concatenate(parts, axis=0)
            outs[i][...] = narrow(dot(sel[i][...], block, 1, 0)).reshape(slots, total // slots, width)

    shapes = [jax.ShapeDtypeStruct((slots, total // slots, width), BF16)] * count
    return call(
        kernel,
        2 * count * total * rows * width,
        2 * count * width * (rows + total),
        in_specs=[full(a) for a in flat + list(picks)],
        out_specs=[full(a) for a in shapes],
        out_shape=shapes,
    )(*flat, *picks)


def rows_of(refs):
    return jnp.concatenate([r[0] for r in refs], axis=0)


def forward(xs, gates, w_in, w_out):
    slots, width, both = w_in.shape
    hidden, count, room = both // 2, len(xs), xs[0].shape[1]
    total = count * room

    def kernel(*refs):
        x_refs, g_refs = refs[:count], refs[count : 2 * count]
        wi_ref, wo_ref, out_ref, act_ref, lr_ref = refs[2 * count :]
        weight = rows_of(g_refs)[:, :1]
        pre = dot(rows_of(x_refs), wi_ref[0], 1, 0)
        gate, up = pre[:, :hidden], pre[:, hidden:]
        sig = jax.nn.sigmoid(gate)
        lean = weight * (gate * sig)
        act = narrow(lean * up)
        act_ref[0] = act
        lr_ref[0, :, :hidden] = weight * up * sig * (1.0 + gate * (1.0 - sig))
        lr_ref[0, :, hidden:] = lean
        out_ref[0] = narrow(dot(act, wo_ref[0], 1, 0)).reshape(count, room, width)

    at = lambda s: (s, 0, 0)
    shapes = [
        jax.ShapeDtypeStruct((slots, count, room, width), BF16),
        jax.ShapeDtypeStruct((slots, total, hidden), BF16),
        jax.ShapeDtypeStruct((slots, total, both), F32),
    ]
    return call(
        kernel,
        2 * slots * total * width * (both + hidden),
        2 * slots * width * (2 * total + both + hidden),
        grid=(slots,),
        in_specs=[pl.BlockSpec((1, room, width), at)] * count
        + [pl.BlockSpec((1, room, LANES), at)] * count
        + [pl.BlockSpec((1, width, both), at), pl.BlockSpec((1, hidden, width), at)],
        out_specs=[
            pl.BlockSpec((1, count, room, width), lambda s: (s, 0, 0, 0)),
            pl.BlockSpec((1, total, hidden), at),
            pl.BlockSpec((1, total, both), at),
        ],
        out_shape=shapes,
    )(*xs, *gates, w_in, w_out)


def backward(ds, lrs, w_out, first, last, lean):
    count, (slots, room, width) = len(ds), ds[0].shape
    hidden, both = w_out.shape[1], lrs[0].shape[2]
    total, here = count * room, last - first

    def kernel(*refs):
        d_refs = refs[:count]
        w_ref, all_ref, lean_ref = refs[count + len(lrs) :]
        d_act = dot(rows_of(d_refs), w_ref[0], 1, 1)
        lr = rows_of(refs[count : count + len(lrs)])
        d_pre = jnp.concatenate([d_act * lr[:, :hidden], d_act * lr[:, hidden:]], axis=1)
        all_ref[0] = narrow(d_pre)
        rows = d_pre.reshape(count, room, both)[:, :lean].reshape(count * lean, both)
        lean_ref[0] = narrow(rows)

    at = lambda s: (s + first, 0, 0)
    return call(
        kernel,
        2 * here * total * width * hidden,
        2 * here * width * (total + hidden),
        grid=(here,),
        in_specs=[pl.BlockSpec((1, room, width), at)] * count
        + [pl.BlockSpec((1, total // len(lrs), both), at)] * len(lrs)
        + [pl.BlockSpec((1, hidden, width), at)],
        out_specs=[
            pl.BlockSpec((1, total, both), lambda s: (s, 0, 0)),
            pl.BlockSpec((1, count * lean, both), lambda s: (s, 0, 0)),
        ],
        out_shape=[
            jax.ShapeDtypeStruct((here, total, both), BF16),
            jax.ShapeDtypeStruct((here, count * lean, both), BF16),
        ],
    )(*ds, *lrs, w_out)


def out_gradients(ds, acts, order, parts, first, here):
    count, (_, room, width) = len(ds), ds[0].shape
    total, hidden = count * room, acts[0].shape[2]
    part, half = width // parts, parts // 2

    def kernel(*refs):
        order_ref, d_refs = refs[0], refs[1 : 1 + count]
        act_refs, (first_ref, second_ref, whole) = refs[1 + count : -3], refs[-3:]
        whole[...] = narrow(dot(rows_of(act_refs), rows_of(d_refs), 0, 0))
        for j in range(parts):
            cols = pl.ds(pl.multiple_of(order_ref[j] * part, part), part)
            (first_ref if j < half else second_ref)[j % half, 0] = whole[:, cols]

    shape = jax.ShapeDtypeStruct((half, here, hidden, part), BF16)
    spec = pl.BlockSpec((half, 1, hidden, part), lambda s, o: (0, s, 0, 0))
    return call(
        kernel,
        2 * here * total * width * hidden,
        2 * here * width * (total + hidden),
        grid_spec=pltpu.PrefetchScalarGridSpec(
            num_scalar_prefetch=1,
            grid=(here,),
            in_specs=[pl.BlockSpec((1, room, width), lambda s, o: (s + first, 0, 0))] * count
            + [pl.BlockSpec((1, total // len(acts), hidden), lambda s, o: (s + first, 0, 0))] * len(acts),
            out_specs=[spec, spec],
            scratch_shapes=[pltpu.VMEM((hidden, width), BF16)],
        ),
        out_shape=[shape, shape],
    )(order, *ds, *acts)


def finish(piece, index, slots, into):
    here, hidden, part = piece[2].shape
    shape = jax.ShapeDtypeStruct((slots, hidden, part), BF16)

    def kernel(keep, got, away, *refs):
        refs[-1][...] = narrow(wide(keep[0]) + wide(got[0]) + wide(away[...]))

    own = pl.BlockSpec((1, here, hidden, part), lambda *_: (1, 0, 0, 0))
    return call(
        kernel,
        3 * here * hidden * part,
        8 * here * hidden * part,
        grid=(1,),
        in_specs=[own, own, full(piece[2])] + ([] if into is None else [pl.BlockSpec(memory_space=pl.ANY)]),
        out_specs=pl.BlockSpec((here, hidden, part), lambda *_: (index, 0, 0)),
        out_shape=shape,
        input_output_aliases={} if into is None else {3: 0},
    )(*piece, *([] if into is None else [into]))


def in_gradients(xs, d_pres, first, last, into):
    slots, half_rows, part = xs[0].shape
    both, groups = d_pres[0].shape[2], len(d_pres)
    here = last - first

    def kernel(*refs):
        x = jnp.concatenate([r[0] for r in refs[: 2 * groups]], axis=0)
        d = jnp.concatenate([r[0] for r in refs[2 * groups : 3 * groups]], axis=0)
        refs[-1][0] = narrow(dot(x, d, 0, 0))

    at = lambda s: (s + first, 0, 0)
    return call(
        kernel,
        4 * here * groups * half_rows * part * both,
        4 * here * groups * half_rows * (part + both),
        grid=(here,),
        in_specs=[pl.BlockSpec((1, half_rows, part), at)] * (2 * groups)
        + [pl.BlockSpec((1, 2 * half_rows, both), lambda s: (s, 0, 0))] * groups
        + ([] if into is None else [pl.BlockSpec(memory_space=pl.ANY)]),
        out_specs=pl.BlockSpec((1, part, both), at),
        out_shape=jax.ShapeDtypeStruct((slots, part, both), BF16),
        input_output_aliases={} if into is None else {3 * groups: 0},
    )(*xs, *d_pres, *([] if into is None else [into]))


def rows_back(d_pre, w_in, count, first):
    here, total, both = d_pre.shape
    width = w_in.shape[1]

    def kernel(d_ref, w_ref, out_ref):
        out_ref[0] = narrow(dot(d_ref[0], w_ref[0], 1, 1)).reshape(out_ref.shape[1:])

    return call(
        kernel,
        2 * total * width * here * both,
        2 * width * here * (total + both),
        grid=(here,),
        in_specs=[
            pl.BlockSpec((1, total, both), lambda s: (s, 0, 0)),
            pl.BlockSpec((1, width, both), lambda s: (s + first, 0, 0)),
        ],
        out_specs=pl.BlockSpec((1, count, total // count, width), lambda s: (s, 0, 0, 0)),
        out_shape=jax.ShapeDtypeStruct((here, count, total // count, width), BF16),
    )(d_pre, w_in)


def combine(outs, jobs, shapes):
    width = outs[0][0].shape[3]
    arrays, specs, plan = [], [], []
    for block, pick, addends in jobs:
        count = outs[0][0].shape[1]
        here, block = outs[block // count], block % count
        arrays += [o for o in here] + [pick] + [a for _, a in addends]
        specs += [
            pl.BlockSpec((o.shape[0], 1, o.shape[2], width), lambda *_, b=block: (0, b, 0, 0)) for o in here
        ]
        specs += [full(pick)] + [full(a) for _, a in addends]
        plan.append([at for at, _ in addends])
    out_shapes = [jax.ShapeDtypeStruct((n, width), BF16) for pieces in shapes for _, n in pieces]

    def kernel(*refs):
        ins, res = list(refs[: len(arrays)]), list(refs[len(arrays) :])
        for addends, pieces in zip(plan, shapes):
            rows = jnp.concatenate(
                [ins.pop(0)[...].reshape(-1, width) for _ in outs[0]], axis=0
            )
            acc = dot(ins.pop(0)[...], rows, 0, 0)
            for at in addends:
                more = wide(ins.pop(0)[...])
                if more.shape[0] == acc.shape[0]:
                    acc = acc + more
                else:
                    cut = [acc[:at], acc[at : at + more.shape[0]] + more, acc[at + more.shape[0] :]]
                    acc = jnp.concatenate([c for c in cut if c.shape[0]], axis=0)
            for at, n in pieces:
                res.pop(0)[...] = narrow(acc[at : at + n])

    size = sum(2 * a.size for a in out_shapes)
    return call(
        kernel,
        2 * len(jobs) * jobs[0][1].size * width,
        2 * len(jobs) * jobs[0][1].shape[0] * width + 3 * size,
        grid=(1,),
        in_specs=specs,
        out_specs=[full(a) for a in out_shapes],
        out_shape=out_shapes,
    )(*arrays)


def ring_scatter(outs, picks, pairs):
    ahead, back = pairs
    count, rows = len(ahead), picks[0].shape[1]
    half = rows // 2
    f, g = combine(outs, [(count - 1, picks[-1], [])], [[(0, half), (half, half)]])
    offsets = (0, half)
    for step in range(count // 2 - 1, 0, -1):
        f = lax.ppermute(f, "expert", ahead)
        g = lax.ppermute(g, "expert", back)
        jobs = [(2 * step, picks[2 * step], [(offsets[0], f)]), (2 * step - 1, picks[2 * step - 1], [(offsets[1], g)])]
        f, g = combine(outs, jobs, [[(0, rows)], [(0, rows)]])
        offsets = (0, 0)
    f = lax.ppermute(f, "expert", ahead)
    g = lax.ppermute(g, "expert", back)
    return combine(outs, [(0, picks[0], [(0, f), (0, g)])], [[(0, rows)]])[0]


def ring_scatter_halves(outs, picks, pairs):
    ahead, back = pairs
    count, rows = len(ahead), picks[0].shape[1]
    half, last = rows // 2, len(ahead) // 2
    lows, highs = (0, half), (half, half)
    lf, hg = combine(outs, [(count - 1, picks[-1], [])], [[lows, highs]])
    lg = hf = None
    for stage in range(1, last + 1):
        lf = lax.ppermute(lf, "expert", ahead)
        lg = None if lg is None else lax.ppermute(lg, "expert", back)
        hf = None if hf is None else lax.ppermute(hf, "expert", ahead)
        hg = lax.ppermute(hg, "expert", back)
        if stage == last:
            break
        fwd, bwd = 2 * (last - stage), 2 * (last - stage) - 1
        jobs = lambda at, f, g: [
            (b, picks[b], [] if a is None else [(at, a)]) for b, a in ((fwd, f), (bwd, g))
        ]
        lf, lg = combine(outs, jobs(0, lf, lg), [[lows], [lows]])
        hf, hg = combine(outs, jobs(half, hf, hg), [[highs], [highs]])
    addends = [(0, lf), (0, lg), (half, hf), (half, hg)]
    return combine(outs, [(0, picks[0], addends)], [[(0, rows)]])[0]


def ring_gather(block, pairs):
    ahead, back = pairs
    half = block.shape[0] // 2
    f = g = block
    blocks = [[block]]
    for _ in range(1, len(ahead) // 2):
        f = lax.ppermute(f, "expert", ahead)
        g = lax.ppermute(g, "expert", back)
        blocks += [[f], [g]]
    low = lax.ppermute(f[:half], "expert", ahead)
    high = lax.ppermute(g[half:], "expert", back)
    return blocks + [[low, high]]


def ring_gather_halves(low, high, pairs):
    ahead, back = pairs
    lf = lg = low
    hf = hg = high
    blocks = [[low, high]]
    for _ in range(1, len(ahead) // 2):
        lf = lax.ppermute(lf, "expert", ahead)
        lg = lax.ppermute(lg, "expert", back)
        hf = lax.ppermute(hf, "expert", ahead)
        hg = lax.ppermute(hg, "expert", back)
        blocks += [[lf, hf], [lg, hg]]
    low = lax.ppermute(lf, "expert", ahead)
    high = lax.ppermute(hg, "expert", back)
    return blocks + [[low, high]]


def body(tokens, d_mixed, w_in, w_out, expert_ids, gate_fixed, placement):
    rows, width = tokens.shape
    slots, experts, top = w_out.shape[0], placement.shape[0], expert_ids.shape[1]
    ring, parts = lax.axis_size("expert"), lax.axis_size("dp")
    me_e, me_p = lax.axis_index("expert"), lax.axis_index("dp")
    pairs = ring_pairs(ring)
    most = max(2, 5 * rows * top // (4 * experts))
    room, lean = -(-most // 16) * 16, -(-most // 8) * 8

    core_pairs = [(i, i ^ 1) for i in range(parts)]
    chip_pairs = [(i, (i + parts // 2) % parts) for i in range(parts)]
    far_pairs = [(i, (i ^ 1) + parts // 2 if i < parts // 2 else (i ^ 1) - parts // 2) for i in range(parts)]
    core, far, near = me_p % 2, (me_p // 2 + 1) % 2, me_p // 2
    order = jnp.stack([2 * far + 1 - core, 2 * near + 1 - core, 2 * far + core, 2 * near + core])
    routes = (far_pairs, core_pairs, chip_pairs)

    info = jnp.concatenate([order, (me_e * slots)[None]])
    w_in, w_out = in_hbm(w_in), in_hbm(w_out)
    x_blocks = ring_gather_halves(*pack_rows(tokens, expert_ids, gate_fixed), pairs)
    d_blocks = ring_gather(d_mixed, pairs)

    x_blocks = [[in_hbm(a) for a in block] for block in x_blocks]
    half = ring // 2
    routed, columns = [], []
    for i in range(2):
        got, cols = route_rows(
            x_blocks[i * half : (i + 1) * half], placement, info, slots, room, lean, top, width, parts
        )
        routed += got
        columns.append([lax.ppermute(cols[j], "dp", routes[j]) for j in range(parts - 1)] + [cols[-1]])
    xs, picks, gates = (list(a) for a in zip(*routed))

    pair = slots // 2
    lows = range(0, slots, pair)
    outs, acts, lrs = zip(
        *[forward(xs[i * half : (i + 1) * half], gates[i * half : (i + 1) * half], w_in, w_out) for i in range(2)]
    )
    ds = []
    for low, high in ((0, half), (half, ring - 1), (ring - 1, ring)):
        ds += pick_rows(d_blocks[low:high], picks[low:high], slots)

    d_pres, leans, grads = [], [], []
    for low in lows:
        d_pre, mine = backward(ds, lrs, w_out, low, low + pair, lean)
        d_pres.append(d_pre)
        across = lax.ppermute(mine, "dp", chip_pairs)
        beside = lax.ppermute(mine, "dp", core_pairs)
        both = lax.ppermute(across, "dp", core_pairs)
        leans.append([both, beside, across, mine])
        give, keep = out_gradients(ds, acts, order, parts, low, pair)
        got = lax.ppermute(give, "dp", core_pairs)
        away = lax.ppermute(narrow(wide(keep[0]) + wide(got[0])), "dp", chip_pairs)
        grads.append((keep, got, away))
    grad_out = None
    for i, piece in enumerate(grads):
        grad_out = finish(piece, i, slots, grad_out)
    rows_by_group = [columns[i][j] for j in range(parts) for i in range(2)]
    grad_in = None
    for low, d_lean in zip(lows, leans):
        grad_in = in_gradients(rows_by_group, d_lean, low, low + pair, grad_in)

    mixed = ring_scatter([[o] for o in outs], picks, pairs)
    backs = [rows_back(d_pre, w_in, ring, low) for low, d_pre in zip(lows, d_pres)]
    d_tokens = ring_scatter_halves([backs], picks, pairs)
    return mixed, d_tokens, grad_in, grad_out


def solution(mesh):
    rows, slots = P(("dp", "expert"), None), P("expert", None, None)
    return jax.shard_map(
        body,
        mesh=mesh,
        in_specs=(rows, rows, slots, slots, rows, rows, P()),
        out_specs=(rows, rows, P("expert", "dp", None), P("expert", None, "dp")),
        check_vma=False,
    )
```
